32 devices in a mesh: row: 4 (over y, core), col: 8 (over z, x).
Axes of the slice: x: 2, y: 2, z: 4, core: 2. Of those that a mesh axis runs over, the one named last changes fastest.
Arguments:
- grads: bfloat16 [1024, 8192], P('row', 'col'), may hold values from -64 to 64
Outputs:
- kernel: float32 [1024, 1024], P('row', 'col')
The draws below stay inside these ranges and needn't reach their ends.
All inputs are finite; a program needn't handle non-finite values.
Results may differ from the reference program's by a relative error of at most 0.002.
Values may be sent and summed in bfloat16 or wider, within the bound.
No kernel may reach another device: no remote copies, remote signals or barrier semaphores. Data moves between devices by JAX's collectives and lax.ppermute only.
A program may use at most 64 MiB of HBM per device.

```python
import math
import jax
import jax.numpy as jnp
from jax import lax

K = 8192
BW = 64
N_EX = 1024


def draw_grads(key, part):
    keys = jax.random.split(key, 4)
    layers = K // BW
    noise = jax.random.normal(keys[0], (N_EX, layers, BW), jnp.float32)
    mixing = jnp.eye(BW, dtype=jnp.float32)[None] + 0.6 * jax.random.normal(keys[1], (layers, BW, BW), jnp.float32) / math.sqrt(BW)
    column_scale = jnp.exp(jax.random.uniform(keys[2], (layers, BW), jnp.float32, 0.0, math.log(10.0)))
    row_scale = jnp.exp(jax.random.uniform(keys[3], (N_EX, 1, 1), jnp.float32, math.log(0.5), math.log(2.0)))
    values = jnp.einsum('nlb,lbc->nlc', noise, mixing) * column_scale[None] * row_scale
    return jnp.clip(values, -64.0, 64.0).reshape(N_EX, K).astype(jnp.bfloat16)


def setup_inputs(seed: int = 0) -> dict:
    arg_keys = jax.random.split(jax.random.key(seed), 2)
    grads = draw_grads(jax.random.fold_in(arg_keys[1], 71), 0)
    return dict(grads=grads)


def factor(total, count):
    width = total.shape[-1]
    unit = jnp.eye(width, dtype=jnp.float32)
    fisher = total / count + 0.1 * unit
    lower = jnp.linalg.cholesky(fisher)
    return jax.vmap(lambda matrix: jax.scipy.linalg.solve_triangular(matrix, unit, lower=True))(lower)

def reference(grads):
    count = grads.shape[0]
    layers = grads.reshape(count, K // BW, BW).astype(jnp.float32)
    total = jnp.einsum('nlb,nlc->lbc', layers, layers, precision=lax.Precision.HIGHEST)
    inverse = factor(total, count)
    whitened = jnp.einsum('nlb,lcb->nlc', layers, inverse, precision=lax.Precision.HIGHEST)
    whitened = whitened.astype(jnp.bfloat16).reshape(count, K)
    kernel = jnp.dot(whitened.astype(jnp.float32), whitened.T.astype(jnp.float32), preferred_element_type=jnp.float32)
    return kernel * K ** (-0.5)
```

```python
import functools

import jax
import jax.numpy as jnp
from jax import lax
from jax.experimental import pallas as pl
from jax.experimental.pallas import tpu as pltpu
from jax.sharding import PartitionSpec as P

BW = 64
LANES = 128


def lane_gather(rows, index):
    return jnp.take_along_axis(rows, index, axis=1, mode="promise_in_bounds")


def factor(packed):
    groups = packed.shape[0]
    lane = lax.broadcasted_iota(jnp.int32, (groups, LANES), 1)
    base = jnp.where(lane >= BW, BW, 0)
    column = lane - base
    rows = [packed[:, k, :] for k in range(BW)]
    for j in range(BW):
        row = rows[j]
        pivot = lane_gather(row, base + j)
        here = column == j
        step = jnp.where(here, 1.0, row) * (1.0 / pivot)
        for k in range(j + 1, BW):
            rows[k] = jnp.where(here, 0.0, rows[k]) - lane_gather(row, base + k) * step
        packed[:, j, :] = jnp.where(column < j, row, jnp.where(here, 1.0, 0.0)) * lax.rsqrt(pivot)


def body(me_ref, *refs, slots, peers, total):
    grads = refs[:slots]
    outs = refs[slots : slots + peers]
    packed, white = refs[slots + peers :]
    count, width = grads[0].shape
    groups = width // LANES
    block = outs[0].shape[1]

    lane = lax.broadcasted_iota(jnp.int32, (BW, LANES), 1)
    sub = lax.broadcasted_iota(jnp.int32, (BW, LANES), 0)
    low = lane < BW
    unit = jnp.where(sub == jnp.where(low, lane, lane - BW), 0.1, 0.0)
    for s in range(groups):
        acc = None
        for t in range(slots):
            x = grads[t][:, s * LANES : (s + 1) * LANES]
            part = lax.dot_general(
                x, x, (((0,), (0,)), ((), ())), preferred_element_type=jnp.float32
            )
            acc = part if acc is None else acc + part
        packed[s] = jnp.where(low, acc[:BW], acc[BW:]) * (1.0 / total) + unit

    factor(packed)

    for s in range(groups):
        both = packed[s]
        wide = jnp.concatenate([jnp.where(low, both, 0.0), jnp.where(low, 0.0, both)], axis=0)
        high = wide.astype(jnp.bfloat16)
        rest = (wide - high.astype(jnp.float32)).astype(jnp.bfloat16)
        stacked = jnp.concatenate([high, rest], axis=1)
        for t in range(slots):
            x = grads[t][:, s * LANES : (s + 1) * LANES]
            out = lax.dot_general(
                jnp.concatenate([x, x], axis=1),
                stacked,
                (((1,), (1,)), ((), ())),
                preferred_element_type=jnp.float32,
            )
            white[t * count : (t + 1) * count, s * LANES : (s + 1) * LANES] = out.astype(
                jnp.bfloat16
            )

    mine = white[:count, :]
    for p in range(peers):
        start = pl.multiple_of(me_ref[p], block)
        outs[p][...] = lax.dot_general(
            mine,
            white[pl.ds(start, block), :],
            (((1,), (1,)), ((), ())),
            preferred_element_type=jnp.float32,
        ).astype(outs[p].dtype)


def per_device(grads):
    slots = lax.axis_size("row")
    peers = lax.axis_size("col")
    count, width = grads.shape
    total = count * slots
    block = total // peers

    held = {0: grads}
    bit = slots // 2
    while bit:
        for t in list(held):
            held[t ^ bit] = lax.ppermute(
                held[t], "row", [(i, i ^ bit) for i in range(slots)]
            )
        bit //= 2

    row = lax.axis_index("row")
    col = lax.axis_index("col")
    per_slot = count // block
    peer = col ^ jnp.arange(peers, dtype=jnp.int32)
    starts = ((peer // per_slot) ^ row) * count + (peer % per_slot) * block

    outs = pl.pallas_call(
        functools.partial(body, slots=slots, peers=peers, total=total),
        in_specs=[pl.BlockSpec(memory_space=pltpu.SMEM)]
        + [pl.BlockSpec(memory_space=pltpu.VMEM)] * slots,
        out_specs=[pl.BlockSpec(memory_space=pltpu.VMEM)] * peers,
        out_shape=[
            jax.ShapeDtypeStruct((count, block), jnp.bfloat16 if p else jnp.float32)
            for p in range(peers)
        ],
        scratch_shapes=[
            pltpu.VMEM((width // LANES, BW, LANES), jnp.float32),
            pltpu.VMEM((total, width), jnp.bfloat16),
        ],
    )(starts, *[held[t] for t in range(slots)])

    kernel = outs[0]
    for p in range(1, peers):
        got = lax.ppermute(outs[p], "col", [(i, i ^ p) for i in range(peers)])
        kernel = kernel + got.astype(jnp.float32)
    return kernel * (width * peers) ** (-0.5)


def solution(mesh):
    return jax.shard_map(
        per_device,
        mesh=mesh,
        in_specs=(P("row", "col"),),
        out_specs=P("row", "col"),
        check_vma=False,
    )
```

```python
import functools

import jax
import jax.numpy as jnp
from jax import lax
from jax.experimental import pallas as pl
from jax.experimental.pallas import tpu as pltpu
from jax.sharding import PartitionSpec as P

BW = 64
LANES = 128
SUB = 8
VMEM_LIMIT = 16 << 20


def lane_gather(rows, index):
    return jnp.take_along_axis(rows, index, axis=1, mode="promise_in_bounds")


def gram(x):
    return lax.dot_general(x, x, (((0,), (0,)), ((), ())), preferred_element_type=jnp.float32)


def times_transposed(x, y):
    return lax.dot_general(x, y, (((1,), (1,)), ((), ())), preferred_element_type=jnp.float32)


def fisher_sums(grads, store):
    width = grads[0].shape[1]
    wide = min(2 * LANES, width)
    low = lax.broadcasted_iota(jnp.int32, (BW, LANES), 1) < BW
    for w in range(width // wide):
        x = jnp.concatenate([g[:, w * wide : (w + 1) * wide] for g in grads], axis=0)
        square = gram(x)
        for h in range(wide // LANES):
            at = h * LANES
            tile = square[at : at + LANES, at : at + LANES]
            store(w * (wide // LANES) + h, jnp.where(low, tile[:BW], tile[BW:]))


def broadcast_row(block, i):
    return jnp.broadcast_to(block[i : i + 1, :], block.shape)


def factor(packed):
    lane = lax.broadcasted_iota(jnp.int32, (SUB, LANES), 1)
    sub = lax.broadcasted_iota(jnp.int32, (SUB, LANES), 0)
    base = jnp.where(lane >= BW, BW, 0)
    column = lane - base
    blocks = BW // SUB
    groups = packed.shape[0]
    rows = [[packed[s, b * SUB : (b + 1) * SUB, :] for b in range(blocks)] for s in range(groups)]
    for j in range(0, BW, 2):
        first, i = divmod(j, SUB)
        at0 = column == j
        at1 = column == j + 1
        done = jnp.logical_or(at0, at1)
        for s in range(groups):
            top = rows[s][first]
            col0 = [lane_gather(rows[s][b], base + j) for b in range(first, blocks)]
            col1 = [lane_gather(rows[s][b], base + (j + 1)) for b in range(first, blocks)]
            row0 = broadcast_row(top, i)
            row1 = broadcast_row(top, i + 1)
            pivot0 = broadcast_row(col0[0], i)
            cross = broadcast_row(col0[0], i + 1)
            inv0 = 1.0 / pivot0
            ratio = cross * inv0
            pivot1 = broadcast_row(col1[0], i + 1) - cross * ratio
            inv1 = 1.0 / pivot1
            lead = jnp.where(at0, 1.0, row0)
            row1 = jnp.where(at0, 0.0, row1) - ratio * lead
            step0 = jnp.where(at1, 0.0, lead) * inv0
            step1 = jnp.where(at1, 1.0, row1) * inv1
            last0 = jnp.where(column < j, row0, jnp.where(at0, 1.0, 0.0)) * lax.rsqrt(pivot0)
            last1 = jnp.where(column <= j, row1, jnp.where(at1, 1.0, 0.0)) * lax.rsqrt(pivot1)
            for b in range(first, blocks):
                down0 = col0[b - first]
                down1 = col1[b - first] - ratio * down0
                new = jnp.where(done, 0.0, rows[s][b]) - down0 * step0 - down1 * step1
                if b == first:
                    new = jnp.where(
                        sub > i + 1, new, jnp.where(sub == i, last0, jnp.where(sub == i + 1, last1, top))
                    )
                rows[s][b] = new
    for s in range(groups):
        for b in range(blocks):
            packed[s, b * SUB : (b + 1) * SUB, :] = rows[s][b]


def early_body(*refs):
    *grads, sums = refs

    def store(s, value):
        sums[s] = value

    fisher_sums(grads, store)


def body(sums_ref, *refs, slots, peers, total):
    grads = refs[:slots]
    outs = refs[slots : slots + peers]
    packed, white = refs[slots + peers :]
    count, width = grads[0].shape
    block = outs[0].shape[1]
    groups = width // LANES

    lane = lax.broadcasted_iota(jnp.int32, (BW, LANES), 1)
    sub = lax.broadcasted_iota(jnp.int32, (BW, LANES), 0)
    low = lane < BW
    unit = jnp.where(sub == jnp.where(low, lane, lane - BW), 0.1, 0.0)

    def store(s, value):
        packed[s] = (sums_ref[s] + value) * (1.0 / total) + unit

    fisher_sums(grads[slots // 2 :], store)
    factor(packed)

    wide = min(2 * LANES, width)
    pairs = wide // LANES
    zero = jnp.zeros((BW, LANES), jnp.float32)
    for w in range(width // wide):
        blocks = []
        for h in range(pairs):
            both = packed[w * pairs + h]
            for part in (jnp.where(low, both, 0.0), jnp.where(low, 0.0, both)):
                blocks.append(
                    jnp.concatenate([part if i == h else zero for i in range(pairs)], axis=1)
                )
        inverse = jnp.concatenate(blocks, axis=0)
        high = inverse.astype(jnp.bfloat16)
        rest = (inverse - high.astype(jnp.float32)).astype(jnp.bfloat16)
        for t in range(slots):
            x = grads[t][:, w * wide : (w + 1) * wide]
            out = (times_transposed(x, high) + times_transposed(x, rest)).astype(jnp.bfloat16)
            for h in range(pairs):
                white[w * pairs + h, t * count : (t + 1) * count, :] = out[
                    :, h * LANES : (h + 1) * LANES
                ]

    row = lax.axis_index("row")
    col = lax.axis_index("col")
    per_slot = count // block

    def rows_of(start, size):
        return jnp.concatenate(
            [white[s, pl.ds(start, size), :] for s in range(width // LANES)], axis=1
        )

    mine = rows_of(0, count)
    for first in range(0, peers, 2):
        stacked = []
        for p in (first, first + 1):
            peer = col ^ p
            start = ((peer // per_slot) ^ row) * count + (peer % per_slot) * block
            stacked.append(rows_of(pl.multiple_of(start, block), block))
        out = times_transposed(mine, jnp.concatenate(stacked, axis=0))
        for i in range(2):
            outs[first + i][...] = out[:, i * block : (i + 1) * block].astype(
                outs[first + i].dtype
            )


def per_device(grads):
    slots = lax.axis_size("row")
    peers = lax.axis_size("col")
    count, width = grads.shape
    total = count * slots
    block = total // peers
    groups = width // LANES
    vmem = pl.BlockSpec(memory_space=pltpu.VMEM)
    params = pltpu.CompilerParams(vmem_limit_bytes=VMEM_LIMIT)

    def swap(x, bit):
        return lax.ppermute(x, "row", [(i, i ^ bit) for i in range(slots)])

    far = slots // 2
    held = {0: grads, far: swap(grads, far)}
    bit = far // 2
    while bit:
        for t in list(held):
            held[t ^ bit] = swap(held[t], bit)
        bit //= 2

    near = [held[t] for t in range(far)]
    sums = pl.pallas_call(
        early_body,
        in_specs=[vmem] * far,
        out_specs=vmem,
        out_shape=jax.ShapeDtypeStruct((groups, BW, LANES), jnp.float32),
        compiler_params=params,
    )(*near)

    outs = pl.pallas_call(
        functools.partial(body, slots=slots, peers=peers, total=total),
        in_specs=[vmem] * (slots + 1),
        out_specs=[vmem] * peers,
        out_shape=[
            jax.ShapeDtypeStruct((count, block), jnp.bfloat16 if p else jnp.float32)
            for p in range(peers)
        ],
        scratch_shapes=[
            pltpu.VMEM((groups, BW, LANES), jnp.float32),
            pltpu.VMEM((groups, total, LANES), jnp.bfloat16),
        ],
        compiler_params=params,
    )(sums, *[held[t] for t in range(slots)])

    got = [
        lax.ppermute(outs[p], "col", [(i, i ^ p) for i in range(peers)])
        for p in reversed(range(1, peers))
    ]
    kernel = outs[0]
    for part in got:
        kernel = kernel + part.astype(jnp.float32)
    return kernel * (width * peers) ** (-0.5)


def solution(mesh):
    return jax.shard_map(
        per_device,
        mesh=mesh,
        in_specs=(P("row", "col"),),
        out_specs=P("row", "col"),
        check_vma=False,
    )
```

```python
import functools

import jax
import jax.numpy as jnp
from jax import lax
from jax.experimental import pallas as pl
from jax.experimental.pallas import tpu as pltpu
from jax.sharding import PartitionSpec as P

BW = 64
LANES = 128
SUB = 8
VMEM_LIMIT = 16 << 20


def lane_gather(rows, index):
    return jnp.take_along_axis(rows, index, axis=1, mode="promise_in_bounds")


def gram(x):
    return lax.dot_general(x, x, (((0,), (0,)), ((), ())), preferred_element_type=jnp.float32)


def times(x, y):
    return lax.dot_general(x, y, (((1,), (0,)), ((), ())), preferred_element_type=jnp.float32)


def times_transposed(x, y):
    return lax.dot_general(x, y, (((1,), (1,)), ((), ())), preferred_element_type=jnp.float32)


def fisher_sums(grads, store):
    width = grads[0].shape[1]
    wide = min(2 * LANES, width)
    low = lax.broadcasted_iota(jnp.int32, (BW, LANES), 1) < BW
    for w in range(width // wide):
        x = jnp.concatenate([g[:, w * wide : (w + 1) * wide] for g in grads], axis=0)
        square = gram(x)
        for h in range(wide // LANES):
            at = h * LANES
            tile = square[at : at + LANES, at : at + LANES]
            store(w * (wide // LANES) + h, jnp.where(low, tile[:BW], tile[BW:]))


def broadcast_row(block, i):
    return jnp.broadcast_to(block[i : i + 1, :], block.shape)


def to_lanes(packed, rows, groups):
    low = lax.broadcasted_iota(jnp.int32, (BW, LANES), 1) < BW
    for lo in range(SUB):
        parts = []
        for hi in range(BW // SUB):
            part = packed[pl.ds(hi * SUB + lo, groups, stride=BW), :]
            parts += [part] * (SUB // groups)
        half = jnp.concatenate(parts, axis=0)
        turned = jnp.concatenate([half, half], axis=0).T
        rows[pl.ds(lo, BW, stride=SUB), :] = jnp.where(low, turned[:BW], turned[BW:])


def from_lanes(rows, inverse, groups):
    lane = lax.broadcasted_iota(jnp.int32, (LANES, LANES), 1)
    sub = lax.broadcasted_iota(jnp.int32, (LANES, LANES), 0)
    same = (lane < BW) == (sub < BW)
    for lo in range(SUB):
        half = rows[pl.ds(lo, BW, stride=SUB), :]
        turned = jnp.where(same, jnp.concatenate([half, half], axis=0).T, 0.0)
        for h in range(LANES // BW):
            for hi in range(BW // SUB):
                at = (h * (BW // SUB) + hi) * SUB
                inverse[pl.ds(h * BW + hi * SUB + lo, groups, stride=LANES), :] = turned[
                    at : at + groups
                ]


def factor(rows):
    lane = lax.broadcasted_iota(jnp.int32, (SUB, LANES), 1)
    sub = lax.broadcasted_iota(jnp.int32, (SUB, LANES), 0)
    chunk = (lane // SUB) % (BW // SUB)
    column = chunk * SUB + sub
    base = (lane // BW) * BW + lane % SUB

    def at(k):
        return slice(k * SUB, (k + 1) * SUB)

    for p in range(BW // SUB):
        first = p * SUB
        panel = [rows[at(first + q), :] for q in range(SUB)]
        near = [lane_gather(row, base + first) for row in panel]
        inside = chunk == p
        steps = []
        for q in range(SUB):
            here = column == first + q
            pivot = broadcast_row(near[q], q)
            inv = 1.0 / pivot
            step = jnp.where(here, 1.0, panel[q]) * inv
            near_step = near[q] * inv
            for k in range(q + 1, SUB):
                down = broadcast_row(near[q], k)
                panel[k] = jnp.where(here, 0.0, panel[k]) - down * step
                near[k] = near[k] - down * near_step
            steps.append(jnp.where(jnp.logical_and(inside, sub > q), 0.0, step))
            rows[at(first + q), :] = jnp.where(
                column < first + q, panel[q], jnp.where(here, 1.0, 0.0)
            ) * lax.rsqrt(pivot)
        for hi in range(p + 1, BW // SUB):
            downs = [lane_gather(row, base + hi * SUB) for row in panel]
            for lo in range(SUB):
                k = hi * SUB + lo
                row = jnp.where(inside, 0.0, rows[at(k), :])
                for q in range(SUB):
                    row = row - broadcast_row(downs[q], lo) * steps[q]
                rows[at(k), :] = row


def early_body(*refs):
    *grads, sums = refs

    def store(s, value):
        sums[s] = value

    fisher_sums(grads, store)


def body(sums_ref, *refs, slots, peers, total):
    grads = refs[:slots]
    outs = refs[slots : slots + peers]
    packed, rows, inverse, white = refs[slots + peers :]
    count, width = grads[0].shape
    block = outs[0].shape[1]
    groups = width // LANES

    lane = lax.broadcasted_iota(jnp.int32, (BW, LANES), 1)
    sub = lax.broadcasted_iota(jnp.int32, (BW, LANES), 0)
    unit = jnp.where(sub == lane % BW, 0.1, 0.0)

    def store(s, value):
        packed[s * BW : (s + 1) * BW, :] = (sums_ref[s] + value) * (1.0 / total) + unit

    fisher_sums(grads[slots // 2 :], store)
    to_lanes(packed, rows, groups)
    factor(rows)
    from_lanes(rows, inverse, groups)

    wide = min(2 * LANES, width)
    pairs = wide // LANES
    zero = jnp.zeros((LANES, LANES), jnp.float32)
    for w in range(width // wide):
        blocks = []
        for h in range(pairs):
            s = w * pairs + h
            tile = inverse[s * LANES : (s + 1) * LANES, :]
            blocks.append(jnp.concatenate([tile if i == h else zero for i in range(pairs)], axis=1))
        matrix = jnp.concatenate(blocks, axis=0)
        high = matrix.astype(jnp.bfloat16)
        rest = (matrix - high.astype(jnp.float32)).astype(jnp.bfloat16)
        for t in range(slots):
            x = grads[t][:, w * wide : (w + 1) * wide]
            out = (times(x, high) + times(x, rest)).astype(jnp.bfloat16)
            for h in range(pairs):
                white[w * pairs + h, t * count : (t + 1) * count, :] = out[
                    :, h * LANES : (h + 1) * LANES
                ]

    row = lax.axis_index("row")
    col = lax.axis_index("col")
    per_slot = count // block

    def white_rows(start, size):
        return jnp.concatenate(
            [white[s, pl.ds(start, size), :] for s in range(width // LANES)], axis=1
        )

    mine = white_rows(0, count)
    for first in range(0, peers, 2):
        stacked = []
        for p in (first, first + 1):
            peer = col ^ p
            start = ((peer // per_slot) ^ row) * count + (peer % per_slot) * block
            stacked.append(white_rows(pl.multiple_of(start, block), block))
        out = times_transposed(mine, jnp.concatenate(stacked, axis=0))
        for i in range(2):
            outs[first + i][...] = out[:, i * block : (i + 1) * block].astype(
                outs[first + i].dtype
            )


def per_device(grads):
    slots = lax.axis_size("row")
    peers = lax.axis_size("col")
    count, width = grads.shape
    total = count * slots
    block = total // peers
    groups = width // LANES
    vmem = pl.BlockSpec(memory_space=pltpu.VMEM)
    params = pltpu.CompilerParams(vmem_limit_bytes=VMEM_LIMIT)

    def swap(x, bit):
        return lax.ppermute(x, "row", [(i, i ^ bit) for i in range(slots)])

    far = slots // 2
    held = {0: grads, far: swap(grads, far)}
    bit = far // 2
    while bit:
        for t in list(held):
            held[t ^ bit] = swap(held[t], bit)
        bit //= 2

    near = [held[t] for t in range(far)]
    sums = pl.pallas_call(
        early_body,
        in_specs=[vmem] * far,
        out_specs=vmem,
        out_shape=jax.ShapeDtypeStruct((groups, BW, LANES), jnp.float32),
        compiler_params=params,
    )(*near)

    outs = pl.pallas_call(
        functools.partial(body, slots=slots, peers=peers, total=total),
        in_specs=[vmem] * (slots + 1),
        out_specs=[vmem] * peers,
        out_shape=[
            jax.ShapeDtypeStruct((count, block), jnp.bfloat16 if p else jnp.float32)
            for p in range(peers)
        ],
        scratch_shapes=[
            pltpu.VMEM((groups * BW, LANES), jnp.float32),
            pltpu.VMEM((BW * SUB, LANES), jnp.float32),
            pltpu.VMEM((groups * LANES, LANES), jnp.float32),
            pltpu.VMEM((groups, total, LANES), jnp.bfloat16),
        ],
        compiler_params=params,
    )(sums, *[held[t] for t in range(slots)])

    got = [
        lax.ppermute(outs[p], "col", [(i, i ^ p) for i in range(peers)])
        for p in reversed(range(1, peers))
    ]
    kernel = outs[0]
    for part in got:
        kernel = kernel + part.astype(jnp.float32)
    return kernel * (width * peers) ** (-0.5)


def solution(mesh):
    return jax.shard_map(
        per_device,
        mesh=mesh,
        in_specs=(P("row", "col"),),
        out_specs=P("row", "col"),
        check_vma=False,
    )
```

```python
import functools

import jax
import jax.numpy as jnp
from jax import lax
from jax.experimental import pallas as pl
from jax.experimental.pallas import tpu as pltpu
from jax.sharding import PartitionSpec as P

BW = 64
LANES = 128
SUB = 8
VMEM_LIMIT = 16 << 20


def lane_gather(rows, index):
    return jnp.take_along_axis(rows, index, axis=1, mode="promise_in_bounds")


def gram(x):
    return lax.dot_general(x, x, (((0,), (0,)), ((), ())), preferred_element_type=jnp.float32)


def times(x, y):
    return lax.dot_general(x, y, (((1,), (0,)), ((), ())), preferred_element_type=jnp.float32)


def times_transposed(x, y):
    return lax.dot_general(x, y, (((1,), (1,)), ((), ())), preferred_element_type=jnp.float32)


def fisher_sums(grads, store):
    width = grads[0].shape[1]
    wide = min(2 * LANES, width)
    low = lax.broadcasted_iota(jnp.int32, (BW, LANES), 1) < BW
    for w in range(width // wide):
        x = jnp.concatenate([g[:, w * wide : (w + 1) * wide] for g in grads], axis=0)
        square = gram(x)
        for h in range(wide // LANES):
            at = h * LANES
            tile = square[at : at + LANES, at : at + LANES]
            store(w * (wide // LANES) + h, jnp.where(low, tile[:BW], tile[BW:]))


def broadcast_row(block, i):
    return jnp.broadcast_to(block[i : i + 1, :], block.shape)


def to_lanes(packed, rows, groups):
    low = lax.broadcasted_iota(jnp.int32, (BW, LANES), 1) < BW
    for lo in range(SUB):
        parts = []
        for hi in range(BW // SUB):
            part = packed[pl.ds(hi * SUB + lo, groups, stride=BW), :]
            parts += [part] * (SUB // groups)
        half = jnp.concatenate(parts, axis=0)
        turned = jnp.concatenate([half, half], axis=0).T
        rows[pl.ds(lo, BW, stride=SUB), :] = jnp.where(low, turned[:BW], turned[BW:])


def from_lanes(rows, inverse, groups):
    lane = lax.broadcasted_iota(jnp.int32, (LANES, LANES), 1)
    sub = lax.broadcasted_iota(jnp.int32, (LANES, LANES), 0)
    same = (lane < BW) == (sub < BW)
    for lo in range(SUB):
        half = rows[pl.ds(lo, BW, stride=SUB), :]
        turned = jnp.where(same, jnp.concatenate([half, half], axis=0).T, 0.0)
        for h in range(LANES // BW):
            for hi in range(BW // SUB):
                at = (h * (BW // SUB) + hi) * SUB
                inverse[pl.ds(h * BW + hi * SUB + lo, groups, stride=LANES), :] = turned[
                    at : at + groups
                ]


def factor(rows):
    lane = lax.broadcasted_iota(jnp.int32, (SUB, LANES), 1)
    sub = lax.broadcasted_iota(jnp.int32, (SUB, LANES), 0)
    chunk = (lane // SUB) % (BW // SUB)
    column = chunk * SUB + sub
    base = (lane // BW) * BW + lane % SUB

    def at(k):
        return slice(k * SUB, (k + 1) * SUB)

    for p in range(BW // SUB):
        first = p * SUB
        panel = [rows[at(first + q), :] for q in range(SUB)]
        near = [lane_gather(row, base + first) for row in panel]
        inside = chunk == p
        steps = []
        for q in range(SUB):
            here = column == first + q
            pivot = broadcast_row(near[q], q)
            inv = 1.0 / pivot
            step = jnp.where(here, 1.0, panel[q]) * inv
            near_step = near[q] * inv
            for k in range(q + 1, SUB):
                down = broadcast_row(near[q], k)
                panel[k] = jnp.where(here, 0.0, panel[k]) - down * step
                near[k] = near[k] - down * near_step
            steps.append(jnp.where(jnp.logical_and(inside, sub > q), 0.0, step))
            rows[at(first + q), :] = jnp.where(
                column < first + q, panel[q], jnp.where(here, 1.0, 0.0)
            ) * lax.rsqrt(pivot)
        for hi in range(p + 1, BW // SUB):
            downs = [lane_gather(row, base + hi * SUB) for row in panel]
            for lo in range(SUB):
                k = hi * SUB + lo
                row = jnp.where(inside, 0.0, rows[at(k), :])
                for q in range(SUB):
                    row = row - broadcast_row(downs[q], lo) * steps[q]
                rows[at(k), :] = row


def early_body(*refs):
    *grads, sums = refs

    def store(s, value):
        sums[s] = value

    fisher_sums(grads, store)


def body(sums_ref, *refs, slots, total, kept, lent):
    grads = refs[:slots]
    outs = refs[slots : slots + len(kept)]
    *lent_refs, packed, rows, inverse, white = refs[slots + len(kept) :]
    count, width = grads[0].shape
    block = lent_refs[0].shape[1]
    peers = len(kept) + sum(len(part) for part in lent)
    groups = width // LANES

    lane = lax.broadcasted_iota(jnp.int32, (BW, LANES), 1)
    sub = lax.broadcasted_iota(jnp.int32, (BW, LANES), 0)
    unit = jnp.where(sub == lane % BW, 0.1, 0.0)

    def store(s, value):
        packed[s * BW : (s + 1) * BW, :] = (sums_ref[s] + value) * (1.0 / total) + unit

    fisher_sums(grads[slots // 2 :], store)
    to_lanes(packed, rows, groups)
    factor(rows)
    from_lanes(rows, inverse, groups)

    wide = min(2 * LANES, width)
    pairs = wide // LANES
    zero = jnp.zeros((LANES, LANES), jnp.float32)
    for w in range(width // wide):
        blocks = []
        for h in range(pairs):
            s = w * pairs + h
            tile = inverse[s * LANES : (s + 1) * LANES, :]
            blocks.append(jnp.concatenate([tile if i == h else zero for i in range(pairs)], axis=1))
        matrix = jnp.concatenate(blocks, axis=0)
        high = matrix.astype(jnp.bfloat16)
        rest = (matrix - high.astype(jnp.float32)).astype(jnp.bfloat16)
        for t in range(slots):
            x = grads[t][:, w * wide : (w + 1) * wide]
            out = (times(x, high) + times(x, rest)).astype(jnp.bfloat16)
            for h in range(pairs):
                white[w * pairs + h, t * count : (t + 1) * count, :] = out[
                    :, h * LANES : (h + 1) * LANES
                ]

    row = lax.axis_index("row")
    col = lax.axis_index("col")
    per_slot = count // block

    def white_rows(start, size):
        return jnp.concatenate(
            [white[s, pl.ds(start, size), :] for s in range(width // LANES)], axis=1
        )

    mine = white_rows(0, count)
    for first in range(0, peers, 2):
        stacked = []
        for p in (first, first + 1):
            peer = col ^ p
            start = ((peer // per_slot) ^ row) * count + (peer % per_slot) * block
            stacked.append(white_rows(pl.multiple_of(start, block), block))
        out = times_transposed(mine, jnp.concatenate(stacked, axis=0))
        for i in range(2):
            p = first + i
            part = out[:, i * block : (i + 1) * block]
            if p in kept:
                ref = outs[kept.index(p)]
                ref[...] = part.astype(ref.dtype)
            for ref, ps in zip(lent_refs, lent):
                if p in ps:
                    at = ps.index(p) * count
                    ref[at : at + count, :] = part.astype(ref.dtype)


def per_device(grads):
    slots = lax.axis_size("row")
    peers = lax.axis_size("col")
    count, width = grads.shape
    total = count * slots
    block = total // peers
    groups = width // LANES
    straight = list(range(peers // 2, peers * 3 // 4))
    joint = [p for p in reversed(range(2, peers, 2)) if p not in straight]
    kept = [0] + joint + straight
    lent = [[p + 1 for p in joint], [1]]
    vmem = pl.BlockSpec(memory_space=pltpu.VMEM)
    params = pltpu.CompilerParams(vmem_limit_bytes=VMEM_LIMIT)

    def swap(x, bit):
        return lax.ppermute(x, "row", [(i, i ^ bit) for i in range(slots)])

    far = slots // 2
    held = {0: grads, far: swap(grads, far)}
    bit = far // 2
    while bit:
        for t in list(held):
            held[t ^ bit] = swap(held[t], bit)
        bit //= 2

    near = [held[t] for t in range(far)]
    sums = pl.pallas_call(
        early_body,
        in_specs=[vmem] * far,
        out_specs=vmem,
        out_shape=jax.ShapeDtypeStruct((groups, BW, LANES), jnp.float32),
        compiler_params=params,
    )(*near)

    *outs, urgent, loan = pl.pallas_call(
        functools.partial(body, slots=slots, total=total, kept=kept, lent=lent),
        in_specs=[vmem] * (slots + 1),
        out_specs=[vmem] * (len(kept) + 2),
        out_shape=[
            jax.ShapeDtypeStruct((count, block), jnp.bfloat16 if p in straight else jnp.float32)
            for p in kept
        ]
        + [jax.ShapeDtypeStruct((count * len(part), block), jnp.bfloat16) for part in lent],
        scratch_shapes=[
            pltpu.VMEM((groups * BW, LANES), jnp.float32),
            pltpu.VMEM((BW * SUB, LANES), jnp.float32),
            pltpu.VMEM((groups * LANES, LANES), jnp.float32),
            pltpu.VMEM((groups, total, LANES), jnp.bfloat16),
        ],
        compiler_params=params,
    )(sums, *[held[t] for t in range(slots)])
    own = dict(zip(kept, outs))

    def exchange(x, p):
        return lax.ppermute(x, "col", [(i, i ^ p) for i in range(peers)])

    urgent = exchange(urgent, 1)
    got = [exchange(own[p], p) for p in reversed(straight)]
    loan = exchange(loan, 1)
    borrowed = [
        array[i * count : (i + 1) * count].astype(jnp.float32)
        for array, part in zip((urgent, loan), lent)
        for i in range(len(part))
    ]
    for p, more in zip(joint, borrowed):
        got.append(exchange((own[p] + more).astype(jnp.bfloat16), p))
    kernel = own[0] + borrowed[-1]
    for part in got:
        kernel = kernel + part.astype(jnp.float32)
    return kernel * (width * peers) ** (-0.5)


def solution(mesh):
    return jax.shard_map(
        per_device,
        mesh=mesh,
        in_specs=(P("row", "col"),),
        out_specs=P("row", "col"),
        check_vma=False,
    )
```

```python
import functools

import jax
import jax.numpy as jnp
from jax import lax
from jax.experimental import pallas as pl
from jax.experimental.pallas import tpu as pltpu
from jax.sharding import PartitionSpec as P

BW = 64
LANES = 128
SUB = 8
VMEM_LIMIT = 16 << 20


def lane_gather(rows, index):
    return jnp.take_along_axis(rows, index, axis=1, mode="promise_in_bounds")


def gram(x):
    return lax.dot_general(x, x, (((0,), (0,)), ((), ())), preferred_element_type=jnp.float32)


def times(x, y):
    return lax.dot_general(x, y, (((1,), (0,)), ((), ())), preferred_element_type=jnp.float32)


def times_transposed(x, y):
    return lax.dot_general(x, y, (((1,), (1,)), ((), ())), preferred_element_type=jnp.float32)


def fisher_sums(grads, store):
    width = grads[0].shape[1]
    wide = min(2 * LANES, width)
    low = lax.broadcasted_iota(jnp.int32, (BW, LANES), 1) < BW
    for w in range(width // wide):
        x = jnp.concatenate([g[:, w * wide : (w + 1) * wide] for g in grads], axis=0)
        square = gram(x)
        for h in range(wide // LANES):
            at = h * LANES
            tile = square[at : at + LANES, at : at + LANES]
            store(w * (wide // LANES) + h, jnp.where(low, tile[:BW], tile[BW:]))


def broadcast_row(block, i):
    return jnp.broadcast_to(block[i : i + 1, :], block.shape)


def to_lanes(packed, rows, groups):
    lane = lax.broadcasted_iota(jnp.int32, (BW, LANES), 1)
    even = (lane // SUB) % 2 == 0
    for lo in range(SUB):
        parts = []
        for s in range(SUB):
            part = packed[pl.ds((s % groups) * BW + lo, SUB, stride=SUB), :]
            parts += [part, part]
        turned = jnp.concatenate(parts, axis=0).T
        rows[pl.ds(lo, BW, stride=SUB), :] = jnp.where(even, turned[:BW], turned[BW:])


def from_lanes(rows, inverse, groups):
    low = lax.broadcasted_iota(jnp.int32, (SUB, LANES), 1) < BW
    for lo in range(SUB):
        half = rows[pl.ds(lo, BW, stride=SUB), :]
        turned = jnp.concatenate([half, half], axis=0).T
        for s in range(groups):
            for h in range(2):
                at = (s * 2 + h) * SUB
                tile = turned[at : at + SUB]
                tile = jnp.where(low, 0.0, tile) if h else jnp.where(low, tile, 0.0)
                inverse[pl.ds((s * 2 + h) * BW + lo, SUB, stride=SUB), :] = tile


def factor(rows):
    lane = lax.broadcasted_iota(jnp.int32, (SUB, LANES), 1)
    sub = lax.broadcasted_iota(jnp.int32, (SUB, LANES), 0)
    chunk = lane % SUB
    column = chunk * SUB + sub
    base = lane - chunk

    def at(k):
        return slice(k * SUB, (k + 1) * SUB)

    for p in range(BW // SUB):
        first = p * SUB
        panel = [rows[at(first + q), :] for q in range(SUB)]
        near = [lane_gather(row, base + p) for row in panel]
        inside = chunk == p
        steps = []
        for q in range(SUB):
            here = column == first + q
            pivot = broadcast_row(near[q], q)
            inv = 1.0 / pivot
            step = jnp.where(here, 1.0, panel[q]) * inv
            near_step = near[q] * inv
            for k in range(q + 1, SUB):
                down = broadcast_row(near[q], k)
                panel[k] = jnp.where(here, 0.0, panel[k]) - down * step
                near[k] = near[k] - down * near_step
            steps.append(jnp.where(jnp.logical_and(inside, sub > q), 0.0, step))
            rows[at(first + q), :] = jnp.where(
                column < first + q, panel[q], jnp.where(here, 1.0, 0.0)
            ) * lax.rsqrt(pivot)
        for hi in range(p + 1, BW // SUB):
            downs = [lane_gather(row, base + hi) for row in panel]
            for lo in range(SUB):
                k = hi * SUB + lo
                row = jnp.where(inside, 0.0, rows[at(k), :])
                for q in range(SUB):
                    row = row - broadcast_row(downs[q], lo) * steps[q]
                rows[at(k), :] = row


def sums_body(*refs, resumed):
    *grads, sums = refs
    before = grads.pop(0) if resumed else None

    def store(s, value):
        sums[s] = before[s] + value if resumed else value

    fisher_sums(grads, store)


def body(sums_ref, *refs, slots, total, first):
    grads = refs[:slots]
    *refs_out, white, packed, rows, inverse = refs[slots:]
    count, width = grads[0].shape
    groups = width // LANES

    lane = lax.broadcasted_iota(jnp.int32, (BW, LANES), 1)
    sub = lax.broadcasted_iota(jnp.int32, (BW, LANES), 0)
    unit = jnp.where(sub == lane % BW, 0.1, 0.0)

    def store(s, value):
        packed[s * BW : (s + 1) * BW, :] = (sums_ref[s] + value) * (1.0 / total) + unit

    fisher_sums(grads[slots // 2 + 1 :: 2], store)
    to_lanes(packed, rows, groups)
    factor(rows)
    from_lanes(rows, inverse, groups)

    wide = min(2 * LANES, width)
    pairs = wide // LANES
    zero = jnp.zeros((LANES, LANES), jnp.float32)
    for w in range(width // wide):
        blocks = []
        for h in range(pairs):
            s = w * pairs + h
            tile = inverse[s * LANES : (s + 1) * LANES, :]
            blocks.append(jnp.concatenate([tile if i == h else zero for i in range(pairs)], axis=1))
        matrix = jnp.concatenate(blocks, axis=0)
        high = matrix.astype(jnp.bfloat16)
        rest = (matrix - high.astype(jnp.float32)).astype(jnp.bfloat16)
        x = jnp.concatenate([g[:, w * wide : (w + 1) * wide] for g in grads], axis=0)
        out = (times(x, high) + times(x, rest)).astype(jnp.bfloat16)
        for h in range(pairs):
            white[w * pairs + h] = out[:, h * LANES : (h + 1) * LANES]

    products(white, refs_out, first, count)


def products(white, outs, asked, count):
    groups = white.shape[0]
    block = outs[0].shape[1]
    row = lax.axis_index("row")
    col = lax.axis_index("col")
    per_slot = count // block

    def white_rows(start, size):
        return jnp.concatenate([white[s, pl.ds(start, size), :] for s in range(groups)], axis=1)

    mine = white_rows(0, count)
    places = [(ref, i * count, p) for ref, ps in zip(outs, asked) for i, p in enumerate(ps)]
    for first in range(0, len(places), 2):
        pair = places[first : first + 2]
        stacked = []
        for _, _, p in pair:
            peer = col ^ p
            start = ((peer // per_slot) ^ row) * count + (peer % per_slot) * block
            stacked.append(white_rows(pl.multiple_of(start, block), block))
        out = times_transposed(mine, jnp.concatenate(stacked, axis=0))
        for i, (ref, at, _) in enumerate(pair):
            part = out[:, i * block : (i + 1) * block]
            ref[at : at + count, :] = part.astype(ref.dtype)


def rest_body(white, *outs, asked, count):
    products(white, outs, asked, count)


def per_device(grads):
    slots = lax.axis_size("row")
    peers = lax.axis_size("col")
    count, width = grads.shape
    total = count * slots
    block = total // peers
    groups = width // LANES
    straight = list(range(peers // 2, peers * 3 // 4))
    joint = [p for p in reversed(range(2, peers, 2)) if p not in straight]
    first = [[p + 1 for p in joint]] + [[p] for p in straight]
    second = [[p] for p in joint] + [[0], [1]]
    vmem = pl.BlockSpec(memory_space=pltpu.VMEM)
    params = pltpu.CompilerParams(vmem_limit_bytes=VMEM_LIMIT)

    def swap(x, bit):
        return lax.ppermute(x, "row", [(i, i ^ bit) for i in range(slots)])

    def sums_of(arrays, resumed):
        return pl.pallas_call(
            functools.partial(sums_body, resumed=resumed),
            in_specs=[vmem] * len(arrays),
            out_specs=vmem,
            out_shape=jax.ShapeDtypeStruct((groups, BW, LANES), jnp.float32),
            compiler_params=params,
        )(*arrays)

    far = slots // 2
    held = {0: grads, far: swap(grads, far)}
    bit = far // 2
    while bit:
        for t in list(held):
            held[t ^ bit] = swap(held[t], bit)
        bit //= 2

    sums = sums_of([held[t] for t in range(far)], False)
    sums = sums_of([sums] + [held[t] for t in range(far, slots, 2)], True)

    def results(asked, dtypes):
        return [
            jax.ShapeDtypeStruct((count * len(ps), block), dtype)
            for ps, dtype in zip(asked, dtypes)
        ]

    urgent, *sent, white = pl.pallas_call(
        functools.partial(body, slots=slots, total=total, first=first),
        in_specs=[vmem] * (slots + 1),
        out_specs=[vmem] * (len(first) + 1),
        out_shape=results(first, [jnp.bfloat16] * len(first))
        + [jax.ShapeDtypeStruct((groups, total, LANES), jnp.bfloat16)],
        scratch_shapes=[
            pltpu.VMEM((groups * BW, LANES), jnp.float32),
            pltpu.VMEM((BW * SUB, LANES), jnp.float32),
            pltpu.VMEM((groups * LANES, LANES), jnp.float32),
        ],
        compiler_params=params,
    )(sums, *[held[t] for t in range(slots)])
    *kept, own, loan = pl.pallas_call(
        functools.partial(rest_body, asked=second, count=count),
        in_specs=[vmem],
        out_specs=[vmem] * len(second),
        out_shape=results(second, [jnp.float32] * (len(second) - 1) + [jnp.bfloat16]),
        compiler_params=params,
    )(white)

    def exchange(x, p):
        return lax.ppermute(x, "col", [(i, i ^ p) for i in range(peers)])

    urgent = exchange(urgent, 1)
    got = [exchange(x, p) for p, x in reversed(list(zip(straight, sent)))]
    loan = exchange(loan, 1)
    for i, p in enumerate(joint):
        both = kept[i] + urgent[i * count : (i + 1) * count].astype(jnp.float32)
        got.append(exchange(both.astype(jnp.bfloat16), p))
    kernel = own
    for part in got[: len(straight)]:
        kernel = kernel + part.astype(jnp.float32)
    kernel = lax.optimization_barrier(kernel)
    for part in [*got[len(straight) :], loan]:
        kernel = kernel + part.astype(jnp.float32)
    return kernel * (width * peers) ** (-0.5)


def solution(mesh):
    return jax.shard_map(
        per_device,
        mesh=mesh,
        in_specs=(P("row", "col"),),
        out_specs=P("row", "col"),
        check_vma=False,
    )
```

```python
import functools

import jax
import jax.numpy as jnp
from jax import lax
from jax.experimental import pallas as pl
from jax.experimental.pallas import tpu as pltpu
from jax.sharding import PartitionSpec as P

BW = 64
LANES = 128
SUB = 8
VMEM_LIMIT = 16 << 20


def lane_gather(rows, index):
    return jnp.take_along_axis(rows, index, axis=1, mode="promise_in_bounds")


def gram(x):
    return lax.dot_general(x, x, (((0,), (0,)), ((), ())), preferred_element_type=jnp.float32)


def times(x, y):
    return lax.dot_general(x, y, (((1,), (0,)), ((), ())), preferred_element_type=jnp.float32)


def times_transposed(x, y):
    return lax.dot_general(x, y, (((1,), (1,)), ((), ())), preferred_element_type=jnp.float32)


def fisher_sums(grads, store):
    width = grads[0].shape[1]
    wide = min(2 * LANES, width)
    low = lax.broadcasted_iota(jnp.int32, (BW, LANES), 1) < BW
    for w in range(width // wide):
        x = jnp.concatenate([g[:, w * wide : (w + 1) * wide] for g in grads], axis=0)
        square = gram(x)
        for h in range(wide // LANES):
            at = h * LANES
            tile = square[at : at + LANES, at : at + LANES]
            store(w * (wide // LANES) + h, jnp.where(low, tile[:BW], tile[BW:]))


def broadcast_row(block, i):
    return jnp.broadcast_to(block[i : i + 1, :], block.shape)


def to_lanes(packed, rows, groups):
    lane = lax.broadcasted_iota(jnp.int32, (BW, LANES), 1)
    even = (lane // SUB) % 2 == 0
    for lo in range(SUB):
        parts = []
        for s in range(SUB):
            part = packed[pl.ds((s % groups) * BW + lo, SUB, stride=SUB), :]
            parts += [part, part]
        turned = jnp.concatenate(parts, axis=0).T
        rows[pl.ds(lo, BW, stride=SUB), :] = jnp.where(even, turned[:BW], turned[BW:])


def from_lanes(rows, inverse, groups):
    low = lax.broadcasted_iota(jnp.int32, (SUB, LANES), 1) < BW
    for lo in range(SUB):
        half = rows[pl.ds(lo, BW, stride=SUB), :]
        turned = jnp.concatenate([half, half], axis=0).T
        for s in range(groups):
            for h in range(2):
                at = (s * 2 + h) * SUB
                tile = turned[at : at + SUB]
                tile = jnp.where(low, 0.0, tile) if h else jnp.where(low, tile, 0.0)
                inverse[pl.ds((s * 2 + h) * BW + lo, SUB, stride=SUB), :] = tile


def factor(rows):
    lane = lax.broadcasted_iota(jnp.int32, (SUB, LANES), 1)
    sub = lax.broadcasted_iota(jnp.int32, (SUB, LANES), 0)
    chunk = lane % SUB
    column = chunk * SUB + sub
    base = lane - chunk

    def at(k):
        return slice(k * SUB, (k + 1) * SUB)

    for p in range(BW // SUB):
        first = p * SUB
        panel = [rows[at(first + q), :] for q in range(SUB)]
        near = [lane_gather(row, base + p) for row in panel]
        inside = chunk == p
        panel = [jnp.where(inside, 0.0, row) for row in panel]
        steps = []
        for q in range(SUB):
            pivot = broadcast_row(near[q], q)
            inv = 1.0 / pivot
            lead = jnp.where(column == first + q, 1.0, panel[q])
            step = lead * inv
            near_step = near[q] * inv
            for k in range(q + 1, SUB):
                down = broadcast_row(near[q], k)
                panel[k] = panel[k] - down * step
                near[k] = near[k] - down * near_step
            steps.append(step)
            rows[at(first + q), :] = jnp.where(chunk > p, 0.0, lead) * lax.rsqrt(pivot)
        for hi in range(p + 1, BW // SUB):
            downs = [lane_gather(row, base + hi) for row in panel]
            for lo in range(SUB):
                k = hi * SUB + lo
                row = jnp.where(inside, 0.0, rows[at(k), :])
                for q in range(SUB):
                    row = row - broadcast_row(downs[q], lo) * steps[q]
                rows[at(k), :] = row


def sums_body(*refs):
    *grads, sums = refs

    def store(s, value):
        sums[s] = value

    fisher_sums(grads, store)


def factor_body(*refs, total):
    *sums, inverse, packed, rows = refs
    groups = sums[0].shape[0]
    lane = lax.broadcasted_iota(jnp.int32, (BW, LANES), 1)
    sub = lax.broadcasted_iota(jnp.int32, (BW, LANES), 0)
    unit = jnp.where(sub == lane % BW, 0.1, 0.0)
    for s in range(groups):
        whole = sums[0][s]
        for more in sums[1:]:
            whole = whole + more[s]
        packed[s * BW : (s + 1) * BW, :] = whole * (1.0 / total) + unit
    to_lanes(packed, rows, groups)
    factor(rows)
    from_lanes(rows, inverse, groups)


def body(inverse, *refs, slots, first):
    grads = refs[:slots]
    *refs_out, white = refs[slots:]
    count, width = grads[0].shape

    wide = min(2 * LANES, width)
    pairs = wide // LANES
    zero = jnp.zeros((LANES, LANES), jnp.float32)
    for w in range(width // wide):
        blocks = []
        for h in range(pairs):
            s = w * pairs + h
            tile = inverse[s * LANES : (s + 1) * LANES, :]
            blocks.append(jnp.concatenate([tile if i == h else zero for i in range(pairs)], axis=1))
        matrix = jnp.concatenate(blocks, axis=0)
        high = matrix.astype(jnp.bfloat16)
        rest = (matrix - high.astype(jnp.float32)).astype(jnp.bfloat16)
        both = jnp.concatenate([high, rest], axis=0)
        for t in range(slots):
            x = grads[t][:, w * wide : (w + 1) * wide]
            out = times(jnp.concatenate([x, x], axis=1), both).astype(jnp.bfloat16)
            for h in range(pairs):
                white[w * pairs + h, t * count : (t + 1) * count, :] = out[:, h * LANES : (h + 1) * LANES]

    products(white, refs_out, first, count)


def products(white, outs, asked, count):
    groups = white.shape[0]
    block = outs[0].shape[1]
    row = lax.axis_index("row")
    col = lax.axis_index("col")
    per_slot = count // block

    def white_rows(start, size):
        return jnp.concatenate([white[s, pl.ds(start, size), :] for s in range(groups)], axis=1)

    mine = white_rows(0, count)
    places = [(ref, i * count, p) for ref, ps in zip(outs, asked) for i, p in enumerate(ps)]
    for first in range(0, len(places), 2):
        pair = places[first : first + 2]
        stacked = []
        for _, _, p in pair:
            peer = col ^ p
            start = ((peer // per_slot) ^ row) * count + (peer % per_slot) * block
            stacked.append(white_rows(pl.multiple_of(start, block), block))
        out = times_transposed(mine, jnp.concatenate(stacked, axis=0))
        for i, (ref, at, _) in enumerate(pair):
            part = out[:, i * block : (i + 1) * block]
            ref[at : at + count, :] = part.astype(ref.dtype)


def rest_body(white, *outs, asked, count):
    products(white, outs, asked, count)


def per_device(grads):
    slots = lax.axis_size("row")
    peers = lax.axis_size("col")
    count, width = grads.shape
    total = count * slots
    block = total // peers
    groups = width // LANES
    straight = list(range(peers // 2, peers * 3 // 4))
    joint = [p for p in reversed(range(2, peers, 2)) if p not in straight]
    first = [[p + 1 for p in joint]] + [[p] for p in straight]
    second = [[p] for p in joint] + [[0], [1]]
    vmem = pl.BlockSpec(memory_space=pltpu.VMEM)
    params = pltpu.CompilerParams(vmem_limit_bytes=VMEM_LIMIT)

    def swap(x, bit):
        return lax.ppermute(x, "row", [(i, i ^ bit) for i in range(slots)])

    def sums_of(arrays):
        return pl.pallas_call(
            sums_body,
            in_specs=[vmem] * len(arrays),
            out_specs=vmem,
            out_shape=jax.ShapeDtypeStruct((groups, BW, LANES), jnp.float32),
            compiler_params=params,
        )(*arrays)

    far = slots // 2
    held = {0: grads, far: swap(grads, far)}
    bit = far // 2
    while bit:
        for t in list(held):
            held[t ^ bit] = swap(held[t], bit)
        bit //= 2

    sums = [sums_of([held[t] for t in range(far)])]
    sums.append(sums_of([held[t] for t in range(far, slots, 2)]))
    sums.append(swap(sums[1], 1))
    inverse = pl.pallas_call(
        functools.partial(factor_body, total=total),
        in_specs=[vmem] * len(sums),
        out_specs=vmem,
        out_shape=jax.ShapeDtypeStruct((groups * LANES, LANES), jnp.float32),
        scratch_shapes=[
            pltpu.VMEM((groups * BW, LANES), jnp.float32),
            pltpu.VMEM((BW * SUB, LANES), jnp.float32),
        ],
        compiler_params=params,
    )(*sums)

    def results(asked, dtypes):
        return [
            jax.ShapeDtypeStruct((count * len(ps), block), dtype)
            for ps, dtype in zip(asked, dtypes)
        ]

    urgent, *sent, white = pl.pallas_call(
        functools.partial(body, slots=slots, first=first),
        in_specs=[vmem] * (slots + 1),
        out_specs=[vmem] * (len(first) + 1),
        out_shape=results(first, [jnp.bfloat16] * len(first))
        + [jax.ShapeDtypeStruct((groups, total, LANES), jnp.bfloat16)],
        compiler_params=params,
    )(inverse, *[held[t] for t in range(slots)])
    *kept, own, loan = pl.pallas_call(
        functools.partial(rest_body, asked=second, count=count),
        in_specs=[vmem],
        out_specs=[vmem] * len(second),
        out_shape=results(second, [jnp.float32] * (len(second) - 1) + [jnp.bfloat16]),
        compiler_params=params,
    )(white)

    def exchange(x, p):
        return lax.ppermute(x, "col", [(i, i ^ p) for i in range(peers)])

    urgent = exchange(urgent, 1)
    got = [exchange(x, p) for p, x in reversed(list(zip(straight, sent)))]
    loan = exchange(loan, 1)
    for i, p in enumerate(joint):
        both = kept[i] + urgent[i * count : (i + 1) * count].astype(jnp.float32)
        got.append(exchange(both.astype(jnp.bfloat16), p))
    kernel = own
    for part in got[: len(straight)]:
        kernel = kernel + part.astype(jnp.float32)
    kernel = lax.optimization_barrier(kernel)
    for part in [*got[len(straight) :], loan]:
        kernel = kernel + part.astype(jnp.float32)
    return kernel * (width * peers) ** (-0.5)


def solution(mesh):
    return jax.shard_map(
        per_device,
        mesh=mesh,
        in_specs=(P("row", "col"),),
        out_specs=P("row", "col"),
        check_vma=False,
    )
```

```python
import functools

import jax
import jax.numpy as jnp
from jax import lax
from jax.experimental import pallas as pl
from jax.experimental.pallas import tpu as pltpu
from jax.sharding import PartitionSpec as P

BW = 64
LANES = 128
SUB = 8
VMEM_LIMIT = 16 << 20


def lane_gather(rows, index):
    return jnp.take_along_axis(rows, index, axis=1, mode="promise_in_bounds")


def gram(x):
    return lax.dot_general(x, x, (((0,), (0,)), ((), ())), preferred_element_type=jnp.float32)


def times(x, y):
    return lax.dot_general(x, y, (((1,), (0,)), ((), ())), preferred_element_type=jnp.float32)


def times_transposed(x, y):
    return lax.dot_general(x, y, (((1,), (1,)), ((), ())), preferred_element_type=jnp.float32)


def fisher_sums(grads, store):
    width = grads[0].shape[1]
    wide = min(2 * LANES, width)
    low = lax.broadcasted_iota(jnp.int32, (BW, LANES), 1) < BW
    for w in range(width // wide):
        x = jnp.concatenate([g[:, w * wide : (w + 1) * wide] for g in grads], axis=0)
        square = gram(x)
        for h in range(wide // LANES):
            at = h * LANES
            tile = square[at : at + LANES, at : at + LANES]
            store(w * (wide // LANES) + h, jnp.where(low, tile[:BW], tile[BW:]))


def broadcast_row(block, i):
    return jnp.broadcast_to(block[i : i + 1, :], block.shape)


def to_lanes(packed, rows, groups):
    lane = lax.broadcasted_iota(jnp.int32, (BW, LANES), 1)
    even = (lane // SUB) % 2 == 0
    for lo in range(SUB):
        parts = []
        for s in range(SUB):
            part = packed[pl.ds((s % groups) * BW + lo, SUB, stride=SUB), :]
            parts += [part, part]
        turned = jnp.concatenate(parts, axis=0).T
        rows[pl.ds(lo, BW, stride=SUB), :] = jnp.where(even, turned[:BW], turned[BW:])


def from_lanes(rows, inverse, groups):
    low = lax.broadcasted_iota(jnp.int32, (SUB, LANES), 1) < BW
    for lo in range(SUB):
        half = rows[pl.ds(lo, BW, stride=SUB), :]
        turned = jnp.concatenate([half, half], axis=0).T
        for s in range(groups):
            for h in range(2):
                at = (s * 2 + h) * SUB
                tile = turned[at : at + SUB]
                tile = jnp.where(low, 0.0, tile) if h else jnp.where(low, tile, 0.0)
                inverse[pl.ds((s * 2 + h) * BW + lo, SUB, stride=SUB), :] = tile


def factor(rows):
    lane = lax.broadcasted_iota(jnp.int32, (SUB, LANES), 1)
    sub = lax.broadcasted_iota(jnp.int32, (SUB, LANES), 0)
    chunk = lane % SUB
    column = chunk * SUB + sub
    base = lane - chunk

    def at(k):
        return slice(k * SUB, (k + 1) * SUB)

    for p in range(BW // SUB):
        first = p * SUB
        panel = [rows[at(first + q), :] for q in range(SUB)]
        near = [lane_gather(row, base + p) for row in panel]
        inside = chunk == p
        panel = [jnp.where(inside, 0.0, row) for row in panel]
        steps = []
        for q in range(SUB):
            pivot = broadcast_row(near[q], q)
            inv = 1.0 / pivot
            lead = jnp.where(column == first + q, 1.0, panel[q])
            step = lead * inv
            near_step = near[q] * inv
            for k in range(q + 1, SUB):
                down = broadcast_row(near[q], k)
                panel[k] = panel[k] - down * step
                near[k] = near[k] - down * near_step
            steps.append(step)
            rows[at(first + q), :] = jnp.where(chunk > p, 0.0, lead) * lax.rsqrt(pivot)
        for hi in range(p + 1, BW // SUB):
            downs = [lane_gather(row, base + hi) for row in panel]
            for lo in range(SUB):
                k = hi * SUB + lo
                row = jnp.where(inside, 0.0, rows[at(k), :])
                for q in range(SUB):
                    row = row - broadcast_row(downs[q], lo) * steps[q]
                rows[at(k), :] = row


def sums_body(*refs):
    *grads, sums = refs

    def store(s, value):
        sums[s] = value

    fisher_sums(grads, store)


def factor_body(*refs, total):
    *sums, inverse, packed, rows = refs
    groups = sums[0].shape[0]
    lane = lax.broadcasted_iota(jnp.int32, (BW, LANES), 1)
    sub = lax.broadcasted_iota(jnp.int32, (BW, LANES), 0)
    unit = jnp.where(sub == lane % BW, 0.1, 0.0)
    for s in range(groups):
        whole = sums[0][s]
        for more in sums[1:]:
            whole = whole + more[s]
        packed[s * BW : (s + 1) * BW, :] = whole * (1.0 / total) + unit
    to_lanes(packed, rows, groups)
    factor(rows)
    from_lanes(rows, inverse, groups)


def body(inverse, *refs, slots, first):
    grads = refs[:slots]
    *refs_out, white = refs[slots:]
    count, width = grads[0].shape

    wide = min(2 * LANES, width)
    pairs = wide // LANES
    zero = jnp.zeros((LANES, LANES), jnp.float32)
    for w in range(width // wide):
        blocks = []
        for h in range(pairs):
            s = w * pairs + h
            tile = inverse[s * LANES : (s + 1) * LANES, :]
            blocks.append(jnp.concatenate([tile if i == h else zero for i in range(pairs)], axis=1))
        matrix = jnp.concatenate(blocks, axis=0)
        high = matrix.astype(jnp.bfloat16)
        rest = (matrix - high.astype(jnp.float32)).astype(jnp.bfloat16)
        both = jnp.concatenate([high, rest], axis=0)
        for t in range(slots):
            x = grads[t][:, w * wide : (w + 1) * wide]
            out = times(jnp.concatenate([x, x], axis=1), both).astype(jnp.bfloat16)
            for h in range(pairs):
                white[w * pairs + h, t * count : (t + 1) * count, :] = out[:, h * LANES : (h + 1) * LANES]

    products(white, refs_out, first, count)


def products(white, outs, asked, count):
    groups = white.shape[0]
    block = outs[0].shape[1]
    row = lax.axis_index("row")
    col = lax.axis_index("col")
    per_slot = count // block

    def white_rows(start, size):
        return jnp.concatenate([white[s, pl.ds(start, size), :] for s in range(groups)], axis=1)

    mine = white_rows(0, count)
    places = [(ref, i * count, p) for ref, ps in zip(outs, asked) for i, p in enumerate(ps)]
    for first in range(0, len(places), 2):
        pair = places[first : first + 2]
        stacked = []
        for _, _, p in pair:
            peer = col ^ p
            start = ((peer // per_slot) ^ row) * count + (peer % per_slot) * block
            stacked.append(white_rows(pl.multiple_of(start, block), block))
        out = times_transposed(mine, jnp.concatenate(stacked, axis=0))
        for i, (ref, at, _) in enumerate(pair):
            part = out[:, i * block : (i + 1) * block]
            ref[at : at + count, :] = part.astype(ref.dtype)


def rest_body(white, *outs, asked, count):
    products(white, outs, asked, count)


def total_body(*refs, scale):
    *parts, out = refs
    whole = parts[0][...]
    for part in parts[1:]:
        whole = whole + part[...].astype(jnp.float32)
    out[...] = whole * scale


def per_device(grads):
    slots = lax.axis_size("row")
    peers = lax.axis_size("col")
    count, width = grads.shape
    total = count * slots
    block = total // peers
    groups = width // LANES
    straight = list(range(peers // 2, peers * 3 // 4))
    joint = [p for p in reversed(range(2, peers, 2)) if p not in straight]
    first = [[p + 1 for p in joint]] + [[p] for p in straight]
    second = [[p] for p in joint] + [[0], [1]]
    vmem = pl.BlockSpec(memory_space=pltpu.VMEM)
    params = pltpu.CompilerParams(vmem_limit_bytes=VMEM_LIMIT)

    def swap(x, bit):
        return lax.ppermute(x, "row", [(i, i ^ bit) for i in range(slots)])

    def sums_of(arrays):
        return pl.pallas_call(
            sums_body,
            in_specs=[vmem] * len(arrays),
            out_specs=vmem,
            out_shape=jax.ShapeDtypeStruct((groups, BW, LANES), jnp.float32),
            compiler_params=params,
        )(*arrays)

    far = slots // 2
    held = {0: grads, far: swap(grads, far)}
    bit = far // 2
    while bit:
        for t in list(held):
            held[t ^ bit] = swap(held[t], bit)
        bit //= 2

    sums = [sums_of([held[t] for t in range(far)])]
    sums.append(sums_of([held[t] for t in range(far, slots, 2)]))
    sums.append(swap(sums[1], 1))
    inverse = pl.pallas_call(
        functools.partial(factor_body, total=total),
        in_specs=[vmem] * len(sums),
        out_specs=vmem,
        out_shape=jax.ShapeDtypeStruct((groups * LANES, LANES), jnp.float32),
        scratch_shapes=[
            pltpu.VMEM((groups * BW, LANES), jnp.float32),
            pltpu.VMEM((BW * SUB, LANES), jnp.float32),
        ],
        compiler_params=params,
    )(*sums)

    def results(asked, dtypes):
        return [
            jax.ShapeDtypeStruct((count * len(ps), block), dtype)
            for ps, dtype in zip(asked, dtypes)
        ]

    urgent, *sent, white = pl.pallas_call(
        functools.partial(body, slots=slots, first=first),
        in_specs=[vmem] * (slots + 1),
        out_specs=[vmem] * (len(first) + 1),
        out_shape=results(first, [jnp.bfloat16] * len(first))
        + [jax.ShapeDtypeStruct((groups, total, LANES), jnp.bfloat16)],
        compiler_params=params,
    )(inverse, *[held[t] for t in range(slots)])
    *kept, own, loan = pl.pallas_call(
        functools.partial(rest_body, asked=second, count=count),
        in_specs=[vmem],
        out_specs=[vmem] * len(second),
        out_shape=results(second, [jnp.float32] * (len(second) - 1) + [jnp.bfloat16]),
        compiler_params=params,
    )(white)

    def exchange(x, p):
        return lax.ppermute(x, "col", [(i, i ^ p) for i in range(peers)])

    urgent = exchange(urgent, 1)
    got = [exchange(x, p) for p, x in reversed(list(zip(straight, sent)))]
    loan = exchange(loan, 1)
    for i, p in enumerate(joint):
        both = kept[i] + urgent[i * count : (i + 1) * count].astype(jnp.float32)
        got.append(exchange(both.astype(jnp.bfloat16), p))
    kernel = own
    for part in got[: len(straight)]:
        kernel = kernel + part.astype(jnp.float32)
    late = [*got[len(straight) :], loan]
    return pl.pallas_call(
        functools.partial(total_body, scale=(width * peers) ** (-0.5)),
        in_specs=[vmem] * (len(late) + 1),
        out_specs=vmem,
        out_shape=jax.ShapeDtypeStruct((count, block), jnp.float32),
        compiler_params=params,
    )(kernel, *late)


def solution(mesh):
    return jax.shard_map(
        per_device,
        mesh=mesh,
        in_specs=(P("row", "col"),),
        out_specs=P("row", "col"),
        check_vma=False,
    )
```
